32 devices in a mesh: batch: 8 (over z, core), critic: 4 (over y, x).
Axes of the slice: x: 2, y: 2, z: 4, core: 2. Of those that a mesh axis runs over, the one named last changes fastest.
Arguments:
- latents: bfloat16 [64, 16, 4096], P('batch', None, 'critic'), may hold values from -128 to 128
- dest: int32 [64], P('batch'), may hold values from 0 to 63, each once
- ends: int32 [64], P('batch'), may hold values from 1 to 16
- rewards: float32 [64, 16], P('batch'), may hold values from -6 to 6
- actions: int32 [64, 16], P('batch'), may hold values from 0 to 255
- w_in: bfloat16 [4, 4096, 8192], P('critic', None, 'batch'), may hold values from -1 to 1
- b_in: float32 [4, 8192], P('critic', 'batch'), may hold values from -2 to 2
- w_out: bfloat16 [4, 8192, 255], P('critic', 'batch'), may hold values from -2 to 2
- actor_w: bfloat16 [4096, 256], replicated, may hold values from -0.1875 to 0.1875
Outputs:
- critic_values: float32 [4, 64, 16], P('critic', 'batch')
- advantages: float32 [64, 16], P('batch')
- actor_grad: float32 [4096, 256], P(('batch', 'critic'))
The draws below stay inside these ranges and needn't reach their ends.
Inputs may be any that keep to these rules, and one draw needn't show every extreme that they name: `dest`: a permutation of all learner rows.
All inputs are finite; a program needn't handle non-finite values.
Results may differ from the reference program's by a relative error of at most 0.0049.
The reference program's roundings to bfloat16 on the way (of `learner`, `hidden` and `pull`) count: a program that leaves them out, or rounds other values in their place, can miss the bound.
Values may be sent and summed in bfloat16 or wider, within the bound.
A program may use at most 128 MiB of HBM per device.

```python
import jax
import jax.numpy as jnp
from jax import lax

D = 4096
H = 8192
BINS = 255
ACTIONS = 256
HORIZON = 16
TRAJ = 64
CRITICS = 4


spread = 0.01


column_lift = 16.0


def draw_latents(key, part):
    base = jnp.clip(jax.random.normal(jax.random.fold_in(key, 41), (TRAJ, HORIZON, D), jnp.float32), -3.9, 3.9)
    rough = jnp.exp(jax.random.uniform(jax.random.fold_in(key, 42), (TRAJ, HORIZON, 1), jnp.float32, 0.0, 0.693))
    picked = jax.random.randint(jax.random.fold_in(key, 43), (TRAJ, HORIZON, 1), 0, 16)
    level = jax.random.randint(jax.random.fold_in(key, 44), (TRAJ, HORIZON, 1), 0, 3)
    strength = 8.0 * jnp.where(level == 0, 1.0, jnp.where(level == 1, 2.0, 4.0))
    factor = jnp.where(picked == 0, strength, rough)
    return (base * factor).astype(jnp.bfloat16)


def draw_w_in(key, part):
    common = jnp.clip(jax.random.normal(jax.random.fold_in(key, 11), (D, H), jnp.float32), -3.9, 3.9)

    def member(member_key):
        own = jnp.clip(jax.random.normal(member_key, (D, H), jnp.float32), -3.9, 3.9)
        return ((common + spread * own) * D ** (-0.5)).astype(jnp.bfloat16)
    return lax.map(member, jax.random.split(jax.random.fold_in(key, 12), CRITICS))


def draw_b_in(key, part):
    common = jnp.clip(jax.random.normal(jax.random.fold_in(key, 21), (1, H), jnp.float32), -3.9, 3.9)
    own = jnp.clip(jax.random.normal(jax.random.fold_in(key, 22), (CRITICS, H), jnp.float32), -3.9, 3.9)
    return 0.5 * (common + spread * own)


def draw_w_out(key, part):
    common = jnp.clip(jax.random.normal(jax.random.fold_in(key, 31), (H, BINS), jnp.float32), -3.9, 3.9)
    lifted = (jnp.arange(BINS) == 0).astype(jnp.float32)[None, :] * (column_lift / H)

    def member(member_key):
        own = jnp.clip(jax.random.normal(member_key, (H, BINS), jnp.float32), -3.9, 3.9)
        return ((common + spread * own) * (H // 8) ** (-0.5) + lifted).astype(jnp.bfloat16)
    return lax.map(member, jax.random.split(jax.random.fold_in(key, 32), CRITICS))


def place_ends(drawn, rng, least, high):
    spot = [jax.random.randint(jax.random.fold_in(rng, axis), (), 0, length) for axis, length in enumerate(drawn.shape)]
    main_axis = drawn.shape.index(max(drawn.shape))
    next_to = spot[:main_axis] + [(spot[main_axis] + 1) % drawn.shape[main_axis]] + spot[main_axis + 1:]
    return drawn.at[tuple(spot)].set(least).at[tuple(next_to)].set(high)


def level_of(rng, extent, cuts, low, largest):
    def one(dim, parts):
        draws = jax.random.uniform(jax.random.fold_in(jax.random.fold_in(rng, 6), dim), (parts,), jnp.float32, low / len(cuts), largest / len(cuts))
        return jnp.repeat(jnp.exp(draws), extent[dim] // parts).reshape((-1,) + (1,) * (len(extent) - dim - 1))

    level = one(*cuts[0])
    for cut in cuts[1:]:
        level = level * one(*cut)
    return level


def noise(rng, shape, deviation, limit, cuts=(), kind=jnp.bfloat16):
    drawn = jax.random.normal(rng, shape, jnp.float32) * deviation
    if len(cuts) > 0:
        drawn = level_of(rng, shape, cuts, -0.22, 0.18) * drawn
    return jnp.clip(drawn, min=-limit, max=limit).astype(kind)


def setup_inputs(seed: int = 0) -> dict:
    key_list = jax.random.split(jax.random.key(seed), 10)
    latents = draw_latents(jax.random.fold_in(key_list[9], 71), 0)
    dest = jax.random.permutation(key_list[1], TRAJ).astype(jnp.int32)
    ends = place_ends(jax.random.randint(key_list[2], (TRAJ,), 1, HORIZON + 1), jax.random.fold_in(key_list[2], 1), 1, HORIZON).astype(jnp.int32)
    rewards = noise(key_list[3], (TRAJ, HORIZON), 1.0, 6.0, ((0, 8),), jnp.float32)
    actions = place_ends(jax.random.randint(key_list[4], (TRAJ, HORIZON), 0, ACTIONS), jax.random.fold_in(key_list[4], 1), 0, ACTIONS - 1).astype(jnp.int32)
    w_in = draw_w_in(jax.random.fold_in(key_list[9], 71), 0)
    b_in = draw_b_in(jax.random.fold_in(key_list[9], 71), 0)
    w_out = draw_w_out(jax.random.fold_in(key_list[9], 71), 0)
    actor_w = noise(key_list[8], (D, ACTIONS), (D // 4) ** -0.5, 0.1875)
    return dict(latents=latents, dest=dest, ends=ends, rewards=rewards, actions=actions, w_in=w_in, b_in=b_in, w_out=w_out, actor_w=actor_w)


smoothing_heat_factor = 0.2
future_decay_factor = 0.985
blend = 0.95

def reference(latents, dest, ends, rewards, actions, w_in, b_in, w_out, actor_w):
    inverse = jnp.zeros((TRAJ,), jnp.int32).at[dest].set(jnp.arange(TRAJ, dtype=jnp.int32))
    learner = latents[inverse]
    flat = learner.reshape(TRAJ * HORIZON, D)
    bins = -20.0 + 40.0 * jnp.arange(BINS, dtype=jnp.float32) / (BINS - 1)

    def member_value(member):
        weight_a, bias_a, weight_b = member
        hidden = jax.nn.silu(jnp.dot(flat, weight_a, preferred_element_type=jnp.float32) + bias_a).astype(jnp.bfloat16)
        logits = jnp.dot(hidden, weight_b, preferred_element_type=jnp.float32)
        return jnp.dot(jax.nn.softmax(logits, axis=-1), bins)
    judge_estimate_matrix = lax.map(member_value, (w_in, b_in, w_out)).reshape(CRITICS, TRAJ, HORIZON)
    heat_divided_estimate = -judge_estimate_matrix / smoothing_heat_factor
    highest_estimate = lax.optimization_barrier(jnp.max(heat_divided_estimate, axis=0))
    smoothed_lower_bound = -smoothing_heat_factor * (highest_estimate + jnp.log(lax.optimization_barrier(jnp.mean(jnp.exp(heat_divided_estimate - highest_estimate), axis=0))))
    position = jnp.arange(HORIZON, dtype=jnp.int32)
    live = (position[None, :] < ends[:, None]).astype(jnp.float32)
    carry = (position[None, :] + 1 < ends[:, None]).astype(jnp.float32)
    later = smoothed_lower_bound[:, HORIZON - 1]
    columns = [later]
    for index in range(HORIZON - 2, -1, -1):
        later = rewards[:, index] + future_decay_factor * carry[:, index] * ((1.0 - blend) * smoothed_lower_bound[:, index + 1] + blend * later)
        columns.append(later)
    returns = jnp.stack(columns[::-1], axis=1)
    raw = (returns - smoothed_lower_bound) * live
    count = jnp.sum(live)
    scale = jnp.sqrt(jnp.sum(raw * raw) / count + 1e-06)
    advantages = raw / scale
    policy = jax.nn.softmax(jnp.dot(flat, actor_w, preferred_element_type=jnp.float32), axis=-1)
    onehot = (actions.reshape(-1, 1) == jnp.arange(ACTIONS, dtype=jnp.int32)[None, :]).astype(jnp.float32)
    pull = ((policy - onehot) * advantages.reshape(-1, 1) / HORIZON).astype(jnp.bfloat16)
    actor_grad = jnp.dot(flat.T, pull, preferred_element_type=jnp.float32)
    return (judge_estimate_matrix, advantages, actor_grad)
```

```python
import functools

import jax
import jax.numpy as jnp
from jax import lax
from jax.experimental import pallas as pl
from jax.experimental.pallas import tpu as pltpu
from jax.sharding import PartitionSpec as P

smoothing_heat_factor = 0.2
future_decay_factor = 0.985
blend = 0.95
MESH = pl.DeviceIdType.MESH
f32 = jnp.float32
bf16 = jnp.bfloat16
HIGHEST = lax.Precision.HIGHEST


def iota(shape, axis):
    return lax.broadcasted_iota(jnp.int32, shape, axis)


def kernel(
    sizes, lat, dest, ends, rewards, actions, w_hbm, b_in, w_out, aw_hbm,
    cv_out, adv_out, grad_out,
    xbuf, wv, awv, wov, acc, pm, lg, psum, rsib, rz, meta, metabuf, metag,
    vown, vbuf, pay, sbuf, gtmp,
    wsem, lsem, zs, zr, xs, xr, ss, sr, ps, pr, qs, qr, ms, mr, vs, vr, bs, br,
):
    nb, n, ny, nx, horizon, bins_n = sizes
    nz = nb // 2
    rows, cols = lat.shape
    half = rows // 2
    traj = rows // horizon
    total = nb * traj
    b = lax.axis_index("batch")
    c = lax.axis_index("critic")
    z, k = b // 2, b % 2
    y, x = c // nx, c % nx
    sib = z * 2 + (1 - k)
    sends = []

    def batch_peer(d):
        return ((b + d) % nb, c)

    def crit(by, bx):
        return ((y + by) % ny) * nx + (x + bx) % nx

    def weight_copy(rc):
        cc = crit(*rc)
        return (
            pltpu.make_async_copy(
                w_hbm.at[pl.ds(pl.multiple_of(cc * cols, cols), cols)],
                wv.at[pl.ds(pl.multiple_of(cc * cols, cols), cols)],
                wsem.at[rc[0] * nx + rc[1]],
            )
        )

    rel = [(by, bx) for by in range(ny) for bx in range(nx)]
    for rc in rel:
        weight_copy(rc).start()
    aw_copy = pltpu.make_async_copy(aw_hbm, awv, lsem.at[0])
    aw_copy.start()
    own_copy = pltpu.make_async_copy(lat, xbuf.at[z, c, k], lsem.at[1])
    own_copy.start()

    barrier = pltpu.get_barrier_semaphore()
    for d in range(1, nb):
        pl.semaphore_signal(barrier, inc=1, device_id=batch_peer(d), device_id_type=MESH)
    for rc in rel[1:]:
        pl.semaphore_signal(barrier, inc=1, device_id=(b, crit(*rc)), device_id_type=MESH)
    pl.semaphore_wait(barrier, nb - 1 + n - 1)

    def send(src, dst, s, r, dev):
        d = pltpu.make_async_remote_copy(
            src_ref=src, dst_ref=dst, send_sem=s, recv_sem=r, device_id=dev, device_id_type=MESH
        )
        d.start()
        sends.append(d)

    def recv(dst, s, r):
        pltpu.make_async_remote_copy(
            src_ref=dst, dst_ref=dst, send_sem=s, recv_sem=r,
            device_id=(sib, c), device_id_type=MESH,
        ).wait_recv()

    count = [0]

    def zc(dz):
        return (z + dz) % nz

    def hrow(h):
        return pl.ds(h * half, half)

    def xsem(dz, rc, h):
        return (dz * n + rc[0] * nx + rc[1]) * 2 + h

    def ssem(dz, rc):
        return dz * n + rc[0] * nx + rc[1]

    def xsend(dz, rc, h, t):
        at = xbuf.at[zc(dz), crit(*rc), k, hrow(h)]
        src = lat.at[hrow(h)] if dz == 0 and rc == (0, 0) else at
        there = ((rc[0] - t[0]) % ny, (rc[1] - t[1]) % nx)
        send(src, at, xs.at[count[0]], xr.at[xsem(dz, there, h)], (b, crit(*t)))
        count[0] += 1

    def xrecv(dz, rc, h):
        i = xsem(dz, rc, h)
        recv(xbuf.at[zc(dz), crit(*rc), k, hrow(h)], xs.at[0], xr.at[i])

    def relay(dz, rc):
        at = xbuf.at[zc(dz), crit(*rc), k]
        src = lat if dz == 0 and rc == (0, 0) else at
        send(src, at, ss.at[ssem(dz, rc)], sr.at[ssem(dz, rc)], (sib, c))

    def enter(dz):
        if dz > 0:
            recv(xbuf.at[zc(dz), c, k], zs.at[dz], zr.at[dz])
        for o in range(2):
            for tx in range(1, nx):
                xsend(dz, (0, 0), o, (0, tx))
            for ty in range(1, ny):
                xsend(dz, (0, 0), 1 - o, (ty, 0))
        relay(dz, (0, 0))

    def middle(dz):
        for bx in range(1, nx):
            xrecv(dz, (0, bx), 0)
            for ty in range(1, ny):
                xsend(dz, (0, bx), 0, (ty, 0))
        for by in range(1, ny):
            xrecv(dz, (by, 0), 1)
            for tx in range(1, nx):
                xsend(dz, (by, 0), 1, (0, tx))

    def lines(dz):
        for bx in range(1, nx):
            xrecv(dz, (0, bx), 1)
            relay(dz, (0, bx))
        for by in range(1, ny):
            xrecv(dz, (by, 0), 0)
            relay(dz, (by, 0))

    def corners(dz):
        for by in range(1, ny):
            for bx in range(1, nx):
                xrecv(dz, (by, bx), 0)
                xrecv(dz, (by, bx), 1)
                relay(dz, (by, bx))

    hidden_n = wv.shape[1]
    tile = 256

    def product(dz, rc):
        other = xbuf.at[zc(dz), crit(*rc), 1 - k]
        recv(other, ss.at[0], sr.at[ssem(dz, rc)])
        if dz == 0:
            weight_copy(rc).wait()
            if rc == (0, 0):
                own_copy.wait()
                aw_copy.wait()
        first = rc == (0, 0)
        cc = crit(*rc)
        wrows = pl.ds(pl.multiple_of(cc * cols, cols), cols)
        zi = zc(dz)

        def one(i, carry):
            at = pl.ds(pl.multiple_of(i * tile, tile), tile)
            v = jnp.dot(
                xbuf[zi, cc].reshape(2 * rows, cols), wv[wrows, at], preferred_element_type=f32
            )
            if first:
                acc[:, at] = v
            else:
                acc[:, at] += v
            return carry

        lax.fori_loop(0, hidden_n // tile, one, 0)
        v = jnp.dot(
            xbuf[zi, cc].reshape(2 * rows, cols), awv[wrows, :], preferred_element_type=f32
        )
        if first:
            pm[zi] = v
        else:
            pm[zi] += v

    def bins_of(dz):
        hid = jax.nn.silu(acc[...] + b_in[...]).astype(bf16)
        v = jnp.dot(hid, wov[...], preferred_element_type=f32)
        lg[dz] = v.reshape(2, rows, wov.shape[1])
        send(lg.at[dz, 1 - k], rsib.at[dz], ps.at[dz], pr.at[dz], (sib, c))

    def pair_sum(dz):
        recv(rsib.at[dz], ps.at[dz], pr.at[dz])
        psum[dz] = lg[dz, k] + rsib[dz]
        if dz > 0:
            send(psum.at[dz], rz.at[dz], qs.at[dz], qr.at[dz], (zc(dz) * 2 + k, c))

    def spread_rows(m, base):
        t = m.shape[0]
        shape = (t, horizon, m.shape[1])
        keep = iota(shape, 2) == iota(shape, 1) + base
        wide = jnp.where(keep, jnp.broadcast_to(m[:, None, :], shape), 0.0)
        return jnp.sum(wide.reshape(t * horizon, m.shape[1]), axis=-1, keepdims=True)

    def policy(dz):
        zi = zc(dz)
        l = pm[zi]
        e = jnp.exp(l - jnp.max(l, axis=-1, keepdims=True))
        p = e / jnp.sum(e, axis=-1, keepdims=True)
        m = metag[pl.ds(pl.multiple_of(zi * 2 * traj, 2 * traj), 2 * traj), :]
        a = spread_rows(m, horizon)
        hot = (iota(l.shape, 1).astype(f32) == a).astype(f32)
        pm[zi] = p - hot

    def along_z(d):
        send(lat, xbuf.at[z, c, k], zs.at[d], zr.at[d], (zc(nz - d) * 2 + k, c))

    along_z(1)
    enter(0)

    row = iota((traj, 128), 0)
    lane = iota((traj, 128), 1)
    m = jnp.zeros((traj, 128), f32)
    for i in range(traj):
        m = jnp.where((row == i) & (lane == 2 * horizon), ends[i].astype(f32), m)
        m = jnp.where((row == i) & (lane == 2 * horizon + 1), dest[i].astype(f32), m)
    meta[...] = m
    meta[:, 0:horizon] = rewards[...]
    meta[:, horizon : 2 * horizon] = actions[...].astype(f32)
    for d in range(1, nb):
        send(meta, metabuf.at[b], ms.at[d], mr.at[d], batch_peer(d))
    metabuf[b] = meta[...]
    wov[...] = jnp.zeros_like(wov)
    wov[:, 0:bins_n] = w_out[...]

    middle(0)
    if nz > 2:
        along_z(2)
    if nz > 1:
        enter(1)
    lines(0)
    product(0, (0, 0))

    for d in range(1, nb):
        recv(metabuf.at[(b + nb - d) % nb], ms.at[d], mr.at[d])
    everyone = metabuf[...].reshape(total, 128)
    dest_all = everyone[:, 2 * horizon + 1 : 2 * horizon + 2]
    pick = (iota((total, total), 1).astype(f32) == dest_all).astype(f32)
    metag[...] = jnp.dot(pick, everyone, preferred_element_type=f32, precision=HIGHEST)
    mine = (iota((traj, total), 1) == iota((traj, total), 0) + b * traj).astype(f32)
    pick_mine = lax.dot_general(
        mine, pick, (((1,), (1,)), ((), ())), preferred_element_type=f32
    )

    line_blocks = [r for r in rel[1:] if r[0] == 0 or r[1] == 0]
    corner_blocks = [r for r in rel[1:] if r[0] != 0 and r[1] != 0]
    for dz in range(nz):
        if dz > 0:
            product(dz, (0, 0))
        for rc in line_blocks:
            product(dz, rc)
        corners(dz)
        if dz + 1 < nz:
            middle(dz + 1)
            if dz + 3 < nz:
                along_z(dz + 3)
        for rc in corner_blocks:
            product(dz, rc)
        bins_of(dz)
        if dz + 1 < nz:
            lines(dz + 1)
            if dz + 2 < nz:
                enter(dz + 2)
            policy(dz)
            pair_sum(dz)
    pair_sum(nz - 1)
    policy(nz - 1)

    width = grad_out.shape[0]
    start = (b * n + c) * width
    aligned = (start // 128) * 128
    gc = aligned // cols
    goff = pl.multiple_of(aligned % cols, 128)
    xt = xbuf[:, gc, :, :, pl.ds(goff, 128)].reshape(nb * rows, 128).T

    logits = psum[0]
    for d in range(1, nz):
        recv(rz.at[d], qs.at[d], qr.at[d])
        logits = logits + rz[d]
    col = iota(logits.shape, 1)
    real = col < bins_n
    logits = jnp.where(real, logits, -jnp.inf)
    e = jnp.exp(logits - jnp.max(logits, axis=-1, keepdims=True))
    bins = -20.0 + 40.0 * col.astype(f32) / (bins_n - 1)
    value = jnp.sum(e * bins, axis=-1, keepdims=True) / jnp.sum(e, axis=-1, keepdims=True)
    shape = (traj, horizon, 128)
    wide = jnp.broadcast_to(value, (rows, 128)).reshape(shape)
    wide = jnp.where(iota(shape, 2) == iota(shape, 1), wide, 0.0)
    v = jnp.sum(wide, axis=1)
    vown[...] = v
    for i, rc in enumerate(rel[1:]):
        back = ((-rc[0]) % ny) * nx + (-rc[1]) % nx
        send(vown, vbuf.at[back], vs.at[i + 1], vr.at[back], (b, crit(*rc)))
    pay[0] = v
    heats = [-v / smoothing_heat_factor]
    for i in range(1, n):
        recv(vbuf.at[i], vs.at[i], vr.at[i])
        heats.append(-vbuf[i] / smoothing_heat_factor)
    top = functools.reduce(jnp.maximum, heats)
    mean = functools.reduce(jnp.add, [jnp.exp(h - top) for h in heats]) / n
    pay[1] = -smoothing_heat_factor * (top + jnp.log(mean))
    for d in range(1, nb):
        send(pay, sbuf.at[b], bs.at[d], br.at[d], batch_peer(d))
    sbuf[b] = pay[...]
    for d in range(1, nb):
        recv(sbuf.at[(b + nb - d) % nb], bs.at[d], br.at[d])
    values = sbuf[:, 0].reshape(total, 128)
    soft = sbuf[:, 1].reshape(total, 128)

    lane = iota((total, 128), 1)
    step = lane.astype(f32)
    mg = metag[...]
    end = mg[:, 2 * horizon : 2 * horizon + 1]
    live = ((step < end) & (lane < horizon)).astype(f32)
    carry = (step + 1.0 < end).astype(f32)

    def ahead(a, s):
        return pltpu.roll(a, 128 - s, 1)

    decay = future_decay_factor * carry
    inner = lane < horizon - 1
    offset = jnp.where(
        inner,
        mg + decay * (1.0 - blend) * ahead(soft, 1),
        jnp.where(lane == horizon - 1, soft, 0.0),
    )
    factor = jnp.where(inner, decay * blend, 0.0)
    s = 1
    while s < horizon:
        offset = offset + factor * ahead(offset, s)
        factor = factor * ahead(factor, s)
        s *= 2
    raw = jnp.where(lane < horizon, (offset - soft) * live, 0.0)
    square = jnp.sum(jnp.sum(raw * raw, axis=1, keepdims=True), axis=0, keepdims=True)
    lives = jnp.sum(jnp.sum(live, axis=1, keepdims=True), axis=0, keepdims=True)
    scale = jnp.sqrt(square / lives + 1e-06)
    adv = raw / scale

    pull = pm[...].reshape(nb * rows, pm.shape[2]) * spread_rows(adv, 0) / horizon
    grad = jnp.dot(xt, pull.astype(bf16), preferred_element_type=f32)
    if width == 128:
        grad_out[...] = grad
    else:
        gtmp[...] = grad
        grad_out[...] = gtmp[pl.ds(pl.multiple_of(start % 128, width), width), :]
    cv_out[0] = jnp.dot(pick_mine, values, preferred_element_type=f32, precision=HIGHEST)[:, 0:horizon]
    adv_out[...] = jnp.dot(pick_mine, adv, preferred_element_type=f32, precision=HIGHEST)[:, 0:horizon]
    for d in sends:
        d.wait_send()


def plane_kernel(
    sizes, lat, dest, ends, rewards, actions, w_hbm, b_in, w_out, aw_hbm,
    cv_out, adv_out, grad_out,
    xbuf, wv, wov, acc, pm, lg, psum, rsib, rz, meta, metabuf, metag,
    vown, vbuf, pay, sbuf,
    wsem, lsem, zs, zr, xs, xr, ss, sr, ps, pr, qs, qr, ms, mr, vs, vr, bs, br,
):
    nb, n, horizon, bins_n = sizes
    nz = nb // 2
    rows, cols = lat.shape
    half = rows // 2
    traj = rows // horizon
    total = nb * traj
    hidden_n = w_hbm.shape[1]
    acts = aw_hbm.shape[1]
    b = lax.axis_index("batch")
    c = lax.axis_index("critic")
    z, k = b // 2, b % 2
    y, x = c // 2, c % 2
    sib = z * 2 + (1 - k)
    col = [c, y * 2 + (1 - x), (1 - y) * 2 + x, (1 - y) * 2 + (1 - x)]
    sends = []

    def closeness(i):
        side = 1 if i < nz / 2 else -1
        return sorted(range(nz), key=lambda p: (abs(p - i), side * (i - p)))

    def pick(values):
        v = jnp.int32(values[0])
        for i in range(1, nz):
            v = jnp.where(z == i, jnp.int32(values[i]), v)
        return v

    orders = [closeness(i) for i in range(nz)]
    plane = [z] + [pick([orders[i][s] for i in range(nz)]) for s in range(1, nz)]

    def batch_peer(d):
        return ((b + d) % nb, c)

    def wcopy(q):
        at = pl.ds(pl.multiple_of(col[q] * cols, cols), cols)
        return (
            pltpu.make_async_copy(
                w_hbm.at[at], wv.at[at, pl.ds(0, hidden_n)], wsem.at[q]
            ),
            pltpu.make_async_copy(
                aw_hbm.at[at], wv.at[at, pl.ds(hidden_n, acts)], wsem.at[4 + q]
            ),
        )

    for d in wcopy(0):
        d.start()
    own_copy = pltpu.make_async_copy(lat, xbuf.at[z, c, k], lsem.at[0])
    own_copy.start()

    below, above = z > 0, z < nz - 1
    barrier = pltpu.get_barrier_semaphore()

    def greet(dev):
        pl.semaphore_signal(barrier, inc=1, device_id=dev, device_id_type=MESH)

    greet((sib, c))
    greet((b, col[1]))
    greet((b, col[2]))

    @pl.when(below)
    def _():
        greet(((z - 1) * 2 + k, c))

    @pl.when(above)
    def _():
        greet(((z + 1) * 2 + k, c))

    pl.semaphore_wait(barrier, 3 + jnp.where(below, 1, 0) + jnp.where(above, 1, 0))

    def send(src, dst, s, r, dev, when=None):
        d = pltpu.make_async_remote_copy(
            src_ref=src, dst_ref=dst, send_sem=s, recv_sem=r, device_id=dev, device_id_type=MESH
        )
        if when is None:
            d.start()
        else:
            pl.when(when)(d.start)
        sends.append((d, when))

    def recv(dst, s, r):
        pltpu.make_async_remote_copy(
            src_ref=dst, dst_ref=dst, send_sem=s, recv_sem=r,
            device_id=(sib, c), device_id_type=MESH,
        ).wait_recv()

    def hrow(h):
        return pl.ds(h * half, half)

    def block(s, q, h=None):
        if h is None:
            return xbuf.at[plane[s], col[q], k]
        return xbuf.at[plane[s], col[q], k, hrow(h)]

    def across(s, h):
        src = lat.at[hrow(h)] if s == 0 else block(s, 0, h)
        for j in (1, 2):
            i = (s * 3 + (j - 1)) * 2 + h
            send(src, block(s, 0, h), xs.at[i], xr.at[i], (b, col[j]))

    def onward(s):
        for j in (1, 2):
            i = (s * 3 + 2) * 2 + (j - 1)
            at = block(s, 3 - j, j - 1)
            send(at, at, xs.at[i], xr.at[i], (b, col[j]))

    def arrived(s, q):
        for h in range(2):
            i = (s * 3 + (q - 1)) * 2 + h
            recv(block(s, q, h), xs.at[0], xr.at[i])

    def relay(s, q):
        src = lat if s == 0 and q == 0 else block(s, q)
        send(src, block(s, q), ss.at[s * 4 + q], sr.at[s * 4 + q], (sib, c))

    def along(h):
        for j, (dz, ok) in enumerate(((-1, below), (1, above))):
            send(
                lat.at[hrow(h)], xbuf.at[z, c, k, hrow(h)],
                zs.at[j * 2 + h], zr.at[z * 2 + h], ((z + dz) * 2 + k, c), ok,
            )

    def passed(d, h):
        for j, sg in enumerate((-1, 1)):
            p = z + sg * d
            there = (p >= 0) & (p < nz)
            on = z - sg
            at = xbuf.at[p, c, k, hrow(h)]

            @pl.when(there)
            def _():
                recv(at, zs.at[0], zr.at[p * 2 + h])

            if d < nz - 1:
                send(
                    at, at, zs.at[(d * 2 + j) * 2 + h], zr.at[p * 2 + h],
                    (on * 2 + k, c), there & (on >= 0) & (on < nz),
                )

    tile = 256
    tiles = (hidden_n + acts) // tile

    def product(s, q, first=False):
        p, cc = plane[s], col[q]
        recv(xbuf.at[p, cc, 1 - k], ss.at[0], sr.at[s * 4 + q])
        wrows = pl.ds(pl.multiple_of(cc * cols, cols), cols)

        def one(i, carry):
            at = pl.ds(pl.multiple_of(i * tile, tile), tile)
            v = jnp.dot(
                xbuf[p, cc].reshape(2 * rows, cols), wv[wrows, at], preferred_element_type=f32
            )
            if first:
                acc[s, :, at] = v
            else:
                acc[s, :, at] += v
            return carry

        lax.fori_loop(0, tiles, one, 0)

    def bins_of(s):
        hid = jax.nn.silu(acc[s, :, 0:hidden_n] + b_in[...]).astype(bf16)
        v = jnp.dot(hid, wov[...], preferred_element_type=f32)
        lg[s] = v.reshape(2, rows, wov.shape[1])
        send(lg.at[s, 1 - k], rsib.at[s], ps.at[s], pr.at[s], (sib, c))

    def pair_sum(s):
        recv(rsib.at[s], ps.at[s], pr.at[s])
        psum[s] = lg[s, k] + rsib[s]
        if s > 0:
            send(psum.at[s], rz.at[z], qs.at[s], qr.at[z], (plane[s] * 2 + k, c))

    def spread_rows(m, base):
        t = m.shape[0]
        shape = (t, horizon, m.shape[1])
        keep = iota(shape, 2) == iota(shape, 1) + base
        wide = jnp.where(keep, jnp.broadcast_to(m[:, None, :], shape), 0.0)
        return jnp.sum(wide.reshape(t * horizon, m.shape[1]), axis=-1, keepdims=True)

    def policy(s):
        p = plane[s]
        l = acc[s, :, hidden_n : hidden_n + acts]
        e = jnp.exp(l - jnp.max(l, axis=-1, keepdims=True))
        prob = e / jnp.sum(e, axis=-1, keepdims=True)
        m = metag[pl.ds(pl.multiple_of(p * 2 * traj, 2 * traj), 2 * traj), :]
        a = spread_rows(m, horizon)
        hot = (iota(l.shape, 1).astype(f32) == a).astype(f32)
        pm[p] = prob - hot

    along(0)
    across(0, 0)
    relay(0, 0)
    along(1)
    across(0, 1)
    for q in range(1, 4):
        for d in wcopy(q):
            d.start()

    row = iota((traj, 128), 0)
    lane = iota((traj, 128), 1)
    m = jnp.zeros((traj, 128), f32)
    for i in range(traj):
        m = jnp.where((row == i) & (lane == 2 * horizon), ends[i].astype(f32), m)
        m = jnp.where((row == i) & (lane == 2 * horizon + 1), dest[i].astype(f32), m)
    meta[...] = m
    meta[:, 0:horizon] = rewards[...]
    meta[:, horizon : 2 * horizon] = actions[...].astype(f32)
    metabuf[b] = meta[...]
    wov[...] = jnp.zeros_like(wov)
    wov[:, 0:bins_n] = w_out[...]

    def ready(q):
        for d in wcopy(q):
            d.wait()

    own_copy.wait()
    ready(0)
    product(0, 0, True)
    for q in range(1, 4):
        ready(q)
    passed(1, 0)
    across(1, 0)
    passed(1, 1)
    across(1, 1)
    relay(1, 0)
    for q in (1, 2):
        arrived(0, q)
        relay(0, q)
    for s in range(2, nz):
        product(s - 1, 0, True)
        product(s - 2, 1)
        passed(s, 0)
        across(s, 0)
        product(s - 2, 2)
        passed(s, 1)
        across(s, 1)
        relay(s, 0)
        for q in (1, 2):
            arrived(s - 1, q)
            relay(s - 1, q)
    order = [nz - 2] + list(range(1, nz - 2)) + [nz - 1, 0]
    for s in order[:-2]:
        onward(s)
    product(nz - 1, 0, True)
    for d in range(1, nb):
        send(meta, metabuf.at[b], ms.at[d], mr.at[d], batch_peer(d))
    for q in (1, 2):
        product(nz - 2, q)
    for q in (1, 2):
        arrived(nz - 1, q)
        relay(nz - 1, q)
    onward(nz - 1)
    onward(0)

    for d in range(1, nb):
        recv(metabuf.at[(b + nb - d) % nb], ms.at[d], mr.at[d])
    everyone = metabuf[...].reshape(total, 128)
    dest_all = everyone[:, 2 * horizon + 1 : 2 * horizon + 2]
    pickm = (iota((total, total), 1).astype(f32) == dest_all).astype(f32)
    metag[...] = jnp.dot(pickm, everyone, preferred_element_type=f32, precision=HIGHEST)
    mine = (iota((traj, total), 1) == iota((traj, total), 0) + b * traj).astype(f32)
    pick_mine = lax.dot_general(
        mine, pickm, (((1,), (1,)), ((), ())), preferred_element_type=f32
    )
    for q in (1, 2):
        product(nz - 1, q)

    before = None
    for s in order:
        arrived(s, 3)
        relay(s, 3)
        if before is not None:
            pair_sum(before)
        product(s, 3)
        bins_of(s)
        if s != order[-1]:
            policy(s)
        before = s
    policy(before)
    gc = ((b * n + c) * grad_out.shape[0]) // cols
    goff = pl.multiple_of(((b * n + c) * grad_out.shape[0]) % cols, 128)
    xt = xbuf[:, gc, :, :, pl.ds(goff, 128)].reshape(nb * rows, 128).T
    pair_sum(before)

    logits = psum[0]
    for d in range(1, nz):
        o = (z + d) % nz
        recv(rz.at[o], qs.at[0], qr.at[o])
        logits = logits + rz[o]
    lane2 = iota(logits.shape, 1)
    real = lane2 < bins_n
    logits = jnp.where(real, logits, -jnp.inf)
    e = jnp.exp(logits - jnp.max(logits, axis=-1, keepdims=True))
    bins = -20.0 + 40.0 * lane2.astype(f32) / (bins_n - 1)
    value = jnp.sum(e * bins, axis=-1, keepdims=True) / jnp.sum(e, axis=-1, keepdims=True)
    shape = (traj, horizon, 128)
    wide = jnp.broadcast_to(value, (rows, 128)).reshape(shape)
    wide = jnp.where(iota(shape, 2) == iota(shape, 1), wide, 0.0)
    v = jnp.sum(wide, axis=1)
    vown[...] = v
    for i in range(1, n):
        send(vown, vbuf.at[i], vs.at[i], vr.at[i], (b, col[i]))
    pay[0] = v
    heats = [-v / smoothing_heat_factor]
    for i in range(1, n):
        recv(vbuf.at[i], vs.at[i], vr.at[i])
        heats.append(-vbuf[i] / smoothing_heat_factor)
    top = functools.reduce(jnp.maximum, heats)
    mean = functools.reduce(jnp.add, [jnp.exp(h - top) for h in heats]) / n
    pay[1] = -smoothing_heat_factor * (top + jnp.log(mean))
    for d in range(1, nb):
        send(pay, sbuf.at[b], bs.at[d], br.at[d], batch_peer(d))
    sbuf[b] = pay[...]
    for d in range(1, nb):
        recv(sbuf.at[(b + nb - d) % nb], bs.at[d], br.at[d])
    values = sbuf[:, 0].reshape(total, 128)
    soft = sbuf[:, 1].reshape(total, 128)

    lane = iota((total, 128), 1)
    step = lane.astype(f32)
    mg = metag[...]
    end = mg[:, 2 * horizon : 2 * horizon + 1]
    live = ((step < end) & (lane < horizon)).astype(f32)
    carry = (step + 1.0 < end).astype(f32)

    def ahead(a, s):
        return pltpu.roll(a, 128 - s, 1)

    decay = future_decay_factor * carry
    inner = lane < horizon - 1
    offset = jnp.where(
        inner,
        mg + decay * (1.0 - blend) * ahead(soft, 1),
        jnp.where(lane == horizon - 1, soft, 0.0),
    )
    factor = jnp.where(inner, decay * blend, 0.0)
    s = 1
    while s < horizon:
        offset = offset + factor * ahead(offset, s)
        factor = factor * ahead(factor, s)
        s *= 2
    raw = jnp.where(lane < horizon, (offset - soft) * live, 0.0)
    square = jnp.sum(jnp.sum(raw * raw, axis=1, keepdims=True), axis=0, keepdims=True)
    lives = jnp.sum(jnp.sum(live, axis=1, keepdims=True), axis=0, keepdims=True)
    scale = jnp.sqrt(square / lives + 1e-06)
    adv = raw / scale

    pull = pm[...].reshape(nb * rows, pm.shape[2]) * spread_rows(adv, 0) / horizon
    grad_out[...] = jnp.dot(xt, pull.astype(bf16), preferred_element_type=f32)
    cv_out[0] = jnp.dot(pick_mine, values, preferred_element_type=f32, precision=HIGHEST)[:, 0:horizon]
    adv_out[...] = jnp.dot(pick_mine, adv, preferred_element_type=f32, precision=HIGHEST)[:, 0:horizon]
    for d, when in sends:
        if when is None:
            d.wait_send()
        else:
            pl.when(when)(d.wait_send)


def hand_over(cv, adv, grad, cv_out, adv_out, grad_out):
    cv_out[...] = cv[...]
    adv_out[...] = adv[...]
    grad_out[...] = grad[...]


def on_planes(latents, dest, ends, rewards, actions, w_in, b_in, w_out, actor_w):
    nb = lax.axis_size("batch")
    n = lax.axis_size("critic")
    traj, horizon, cols = latents.shape
    rows = traj * horizon
    width, hidden_n = w_in.shape[1:]
    bins_n = w_out.shape[2]
    acts = actor_w.shape[1]
    nz = nb // 2
    lanes = -(-bins_n // 128) * 128
    vmem = pltpu.VMEM
    dma = pltpu.SemaphoreType.DMA
    scratch = [
        vmem((nz, n, 2, rows, cols), bf16),
        vmem((width, hidden_n + acts), bf16),
        vmem((hidden_n, lanes), bf16),
        vmem((nz, 2 * rows, hidden_n + acts), f32),
        vmem((nz, 2 * rows, acts), f32),
        vmem((nz, 2, rows, lanes), f32),
        vmem((nz, rows, lanes), f32),
        vmem((nz, rows, lanes), f32),
        vmem((nz, rows, lanes), f32),
        vmem((traj, 128), f32),
        vmem((nb, traj, 128), f32),
        vmem((nb * traj, 128), f32),
        vmem((traj, 128), f32),
        vmem((n, traj, 128), f32),
        vmem((2, traj, 128), f32),
        vmem((nb, 2, traj, 128), f32),
        dma((2 * n,)), dma((1,)),
        dma((nz * 4,)), dma((nz * 2,)),
        dma((nz * 6,)), dma((nz * 6,)),
        dma((nz * n,)), dma((nz * n,)),
        dma((nz,)), dma((nz,)),
        dma((nz,)), dma((nz,)),
        dma((nb,)), dma((nb,)),
        dma((n,)), dma((n,)),
        dma((nb,)), dma((nb,)),
    ]
    inside = pl.BlockSpec(memory_space=pltpu.VMEM)
    scalar = pl.BlockSpec(memory_space=pltpu.SMEM)
    outside = pl.BlockSpec(memory_space=pl.ANY)
    shapes = (
        jax.ShapeDtypeStruct((1, traj, horizon), f32),
        jax.ShapeDtypeStruct((traj, horizon), f32),
        jax.ShapeDtypeStruct((width // (nb * n), acts), f32),
    )
    out = pl.pallas_call(
        functools.partial(plane_kernel, (nb, n, horizon, bins_n)),
        out_shape=shapes,
        in_specs=[outside, scalar, scalar, inside, inside, outside, inside, inside, outside],
        out_specs=(inside, inside, inside),
        scratch_shapes=scratch,
        compiler_params=pltpu.CompilerParams(
            collective_id=0, has_side_effects=True, vmem_limit_bytes=60 * 1024 * 1024
        ),
    )(
        latents.reshape(rows, cols), dest, ends, rewards, actions,
        w_in[0], b_in, w_out[0], actor_w,
    )
    return pl.pallas_call(
        hand_over, out_shape=shapes, in_specs=[inside] * 3, out_specs=(inside,) * 3
    )(*out)


def on_device(latents, dest, ends, rewards, actions, w_in, b_in, w_out, actor_w):
    nb = lax.axis_size("batch")
    n = lax.axis_size("critic")
    traj, horizon, cols = latents.shape
    rows = traj * horizon
    width, hidden_n = w_in.shape[1:]
    bins_n = w_out.shape[2]
    acts = actor_w.shape[1]
    nx = 1
    while nx * nx * 4 <= n:
        nx *= 2
    ny = n // nx
    if nx * nx < n and nx == 1:
        nx, ny = n, 1
    nz = nb // 2
    lanes = -(-bins_n // 128) * 128
    half_sends = nz * (2 * (nx - 1 + ny - 1) + 2 * (nx - 1) * (ny - 1))
    vmem = pltpu.VMEM
    dma = pltpu.SemaphoreType.DMA
    scratch = [
        vmem((nz, n, 2, rows, cols), bf16),
        vmem((width, hidden_n), bf16),
        vmem((width, acts), bf16),
        vmem((hidden_n, lanes), bf16),
        vmem((2 * rows, hidden_n), f32),
        vmem((nz, 2 * rows, acts), f32),
        vmem((nz, 2, rows, lanes), f32),
        vmem((nz, rows, lanes), f32),
        vmem((nz, rows, lanes), f32),
        vmem((nz, rows, lanes), f32),
        vmem((traj, 128), f32),
        vmem((nb, traj, 128), f32),
        vmem((nb * traj, 128), f32),
        vmem((traj, 128), f32),
        vmem((n, traj, 128), f32),
        vmem((2, traj, 128), f32),
        vmem((nb, 2, traj, 128), f32),
        vmem((128, acts), f32),
        dma((n,)), dma((2,)),
        dma((nz,)), dma((nz,)),
        dma((half_sends,)), dma((nz * n * 2,)),
        dma((nz * n,)), dma((nz * n,)),
        dma((nz,)), dma((nz,)),
        dma((nz,)), dma((nz,)),
        dma((nb,)), dma((nb,)),
        dma((n,)), dma((n,)),
        dma((nb,)), dma((nb,)),
    ]
    inside = pl.BlockSpec(memory_space=pltpu.VMEM)
    scalar = pl.BlockSpec(memory_space=pltpu.SMEM)
    outside = pl.BlockSpec(memory_space=pl.ANY)
    return pl.pallas_call(
        functools.partial(kernel, (nb, n, ny, nx, horizon, bins_n)),
        out_shape=(
            jax.ShapeDtypeStruct((1, traj, horizon), f32),
            jax.ShapeDtypeStruct((traj, horizon), f32),
            jax.ShapeDtypeStruct((width // (nb * n), acts), f32),
        ),
        in_specs=[outside, scalar, scalar, inside, inside, outside, inside, inside, outside],
        out_specs=(inside, inside, inside),
        scratch_shapes=scratch,
        compiler_params=pltpu.CompilerParams(
            collective_id=0, has_side_effects=True, vmem_limit_bytes=60 * 1024 * 1024
        ),
    )(
        latents.reshape(rows, cols), dest, ends, rewards, actions,
        w_in[0], b_in, w_out[0], actor_w,
    )


def solution(mesh):
    placed = (
        P("batch", None, "critic"),
        P("batch"),
        P("batch"),
        P("batch", None),
        P("batch", None),
        P("critic", None, "batch"),
        P("critic", "batch"),
        P("critic", "batch", None),
        P(),
    )
    planes = mesh.shape["batch"] == 8 and mesh.shape["critic"] == 4
    return jax.shard_map(
        on_planes if planes else on_device,
        mesh=mesh,
        in_specs=placed,
        out_specs=(P("critic", "batch", None), P("batch", None), P(("batch", "critic"), None)),
        check_vma=False,
    )
```

```python
import functools

import jax
import jax.numpy as jnp
from jax import lax
from jax.experimental import pallas as pl
from jax.experimental.pallas import tpu as pltpu
from jax.sharding import PartitionSpec as P

smoothing_heat_factor = 0.2
future_decay_factor = 0.985
blend = 0.95
MESH = pl.DeviceIdType.MESH
f32 = jnp.float32
bf16 = jnp.bfloat16
HIGHEST = lax.Precision.HIGHEST


def iota(shape, axis):
    return lax.broadcasted_iota(jnp.int32, shape, axis)


def kernel(
    sizes, lat, dest, ends, rewards, actions, w_hbm, b_in, w_out, aw_hbm,
    cv_out, adv_out, grad_out,
    xbuf, wv, awv, wov, acc, pm, lg, psum, rsib, rz, meta, metabuf, metag,
    vown, vbuf, pay, sbuf, gtmp,
    wsem, lsem, zs, zr, xs, xr, ss, sr, ps, pr, qs, qr, ms, mr, vs, vr, bs, br,
):
    nb, n, ny, nx, horizon, bins_n = sizes
    nz = nb // 2
    rows, cols = lat.shape
    half = rows // 2
    traj = rows // horizon
    total = nb * traj
    b = lax.axis_index("batch")
    c = lax.axis_index("critic")
    z, k = b // 2, b % 2
    y, x = c // nx, c % nx
    sib = z * 2 + (1 - k)
    sends = []

    def batch_peer(d):
        return ((b + d) % nb, c)

    def crit(by, bx):
        return ((y + by) % ny) * nx + (x + bx) % nx

    def weight_copy(rc):
        cc = crit(*rc)
        return (
            pltpu.make_async_copy(
                w_hbm.at[pl.ds(pl.multiple_of(cc * cols, cols), cols)],
                wv.at[pl.ds(pl.multiple_of(cc * cols, cols), cols)],
                wsem.at[rc[0] * nx + rc[1]],
            )
        )

    rel = [(by, bx) for by in range(ny) for bx in range(nx)]
    for rc in rel:
        weight_copy(rc).start()
    aw_copy = pltpu.make_async_copy(aw_hbm, awv, lsem.at[0])
    aw_copy.start()
    own_copy = pltpu.make_async_copy(lat, xbuf.at[z, c, k], lsem.at[1])
    own_copy.start()

    barrier = pltpu.get_barrier_semaphore()
    for d in range(1, nb):
        pl.semaphore_signal(barrier, inc=1, device_id=batch_peer(d), device_id_type=MESH)
    for rc in rel[1:]:
        pl.semaphore_signal(barrier, inc=1, device_id=(b, crit(*rc)), device_id_type=MESH)
    pl.semaphore_wait(barrier, nb - 1 + n - 1)

    def send(src, dst, s, r, dev):
        d = pltpu.make_async_remote_copy(
            src_ref=src, dst_ref=dst, send_sem=s, recv_sem=r, device_id=dev, device_id_type=MESH
        )
        d.start()
        sends.append(d)

    def recv(dst, s, r):
        pltpu.make_async_remote_copy(
            src_ref=dst, dst_ref=dst, send_sem=s, recv_sem=r,
            device_id=(sib, c), device_id_type=MESH,
        ).wait_recv()

    count = [0]

    def zc(dz):
        return (z + dz) % nz

    def hrow(h):
        return pl.ds(h * half, half)

    def xsem(dz, rc, h):
        return (dz * n + rc[0] * nx + rc[1]) * 2 + h

    def ssem(dz, rc):
        return dz * n + rc[0] * nx + rc[1]

    def xsend(dz, rc, h, t):
        at = xbuf.at[zc(dz), crit(*rc), k, hrow(h)]
        src = lat.at[hrow(h)] if dz == 0 and rc == (0, 0) else at
        there = ((rc[0] - t[0]) % ny, (rc[1] - t[1]) % nx)
        send(src, at, xs.at[count[0]], xr.at[xsem(dz, there, h)], (b, crit(*t)))
        count[0] += 1

    def xrecv(dz, rc, h):
        i = xsem(dz, rc, h)
        recv(xbuf.at[zc(dz), crit(*rc), k, hrow(h)], xs.at[0], xr.at[i])

    def relay(dz, rc):
        at = xbuf.at[zc(dz), crit(*rc), k]
        src = lat if dz == 0 and rc == (0, 0) else at
        send(src, at, ss.at[ssem(dz, rc)], sr.at[ssem(dz, rc)], (sib, c))

    def enter(dz):
        if dz > 0:
            recv(xbuf.at[zc(dz), c, k], zs.at[dz], zr.at[dz])
        for o in range(2):
            for tx in range(1, nx):
                xsend(dz, (0, 0), o, (0, tx))
            for ty in range(1, ny):
                xsend(dz, (0, 0), 1 - o, (ty, 0))
        relay(dz, (0, 0))

    def middle(dz):
        for bx in range(1, nx):
            xrecv(dz, (0, bx), 0)
            for ty in range(1, ny):
                xsend(dz, (0, bx), 0, (ty, 0))
        for by in range(1, ny):
            xrecv(dz, (by, 0), 1)
            for tx in range(1, nx):
                xsend(dz, (by, 0), 1, (0, tx))

    def lines(dz):
        for bx in range(1, nx):
            xrecv(dz, (0, bx), 1)
            relay(dz, (0, bx))
        for by in range(1, ny):
            xrecv(dz, (by, 0), 0)
            relay(dz, (by, 0))

    def corners(dz):
        for by in range(1, ny):
            for bx in range(1, nx):
                xrecv(dz, (by, bx), 0)
                xrecv(dz, (by, bx), 1)
                relay(dz, (by, bx))

    hidden_n = wv.shape[1]
    tile = 256

    def product(dz, rc):
        other = xbuf.at[zc(dz), crit(*rc), 1 - k]
        recv(other, ss.at[0], sr.at[ssem(dz, rc)])
        if dz == 0:
            weight_copy(rc).wait()
            if rc == (0, 0):
                own_copy.wait()
                aw_copy.wait()
        first = rc == (0, 0)
        cc = crit(*rc)
        wrows = pl.ds(pl.multiple_of(cc * cols, cols), cols)
        zi = zc(dz)

        def one(i, carry):
            at = pl.ds(pl.multiple_of(i * tile, tile), tile)
            v = jnp.dot(
                xbuf[zi, cc].reshape(2 * rows, cols), wv[wrows, at], preferred_element_type=f32
            )
            if first:
                acc[:, at] = v
            else:
                acc[:, at] += v
            return carry

        lax.fori_loop(0, hidden_n // tile, one, 0)
        v = jnp.dot(
            xbuf[zi, cc].reshape(2 * rows, cols), awv[wrows, :], preferred_element_type=f32
        )
        if first:
            pm[zi] = v
        else:
            pm[zi] += v

    def bins_of(dz):
        hid = jax.nn.silu(acc[...] + b_in[...]).astype(bf16)
        v = jnp.dot(hid, wov[...], preferred_element_type=f32)
        lg[dz] = v.reshape(2, rows, wov.shape[1])
        send(lg.at[dz, 1 - k], rsib.at[dz], ps.at[dz], pr.at[dz], (sib, c))

    def pair_sum(dz):
        recv(rsib.at[dz], ps.at[dz], pr.at[dz])
        psum[dz] = lg[dz, k] + rsib[dz]
        if dz > 0:
            send(psum.at[dz], rz.at[dz], qs.at[dz], qr.at[dz], (zc(dz) * 2 + k, c))

    def spread_rows(m, base):
        t = m.shape[0]
        shape = (t, horizon, m.shape[1])
        keep = iota(shape, 2) == iota(shape, 1) + base
        wide = jnp.where(keep, jnp.broadcast_to(m[:, None, :], shape), 0.0)
        return jnp.sum(wide.reshape(t * horizon, m.shape[1]), axis=-1, keepdims=True)

    def policy(dz):
        zi = zc(dz)
        l = pm[zi]
        e = jnp.exp(l - jnp.max(l, axis=-1, keepdims=True))
        p = e / jnp.sum(e, axis=-1, keepdims=True)
        m = metag[pl.ds(pl.multiple_of(zi * 2 * traj, 2 * traj), 2 * traj), :]
        a = spread_rows(m, horizon)
        hot = (iota(l.shape, 1).astype(f32) == a).astype(f32)
        pm[zi] = p - hot

    def along_z(d):
        send(lat, xbuf.at[z, c, k], zs.at[d], zr.at[d], (zc(nz - d) * 2 + k, c))

    along_z(1)
    enter(0)

    row = iota((traj, 128), 0)
    lane = iota((traj, 128), 1)
    m = jnp.zeros((traj, 128), f32)
    for i in range(traj):
        m = jnp.where((row == i) & (lane == 2 * horizon), ends[i].astype(f32), m)
        m = jnp.where((row == i) & (lane == 2 * horizon + 1), dest[i].astype(f32), m)
    meta[...] = m
    meta[:, 0:horizon] = rewards[...]
    meta[:, horizon : 2 * horizon] = actions[...].astype(f32)
    for d in range(1, nb):
        send(meta, metabuf.at[b], ms.at[d], mr.at[d], batch_peer(d))
    metabuf[b] = meta[...]
    wov[...] = jnp.zeros_like(wov)
    wov[:, 0:bins_n] = w_out[...]

    middle(0)
    if nz > 2:
        along_z(2)
    if nz > 1:
        enter(1)
    lines(0)
    product(0, (0, 0))

    for d in range(1, nb):
        recv(metabuf.at[(b + nb - d) % nb], ms.at[d], mr.at[d])
    everyone = metabuf[...].reshape(total, 128)
    dest_all = everyone[:, 2 * horizon + 1 : 2 * horizon + 2]
    pick = (iota((total, total), 1).astype(f32) == dest_all).astype(f32)
    metag[...] = jnp.dot(pick, everyone, preferred_element_type=f32, precision=HIGHEST)
    mine = (iota((traj, total), 1) == iota((traj, total), 0) + b * traj).astype(f32)
    pick_mine = lax.dot_general(
        mine, pick, (((1,), (1,)), ((), ())), preferred_element_type=f32
    )

    line_blocks = [r for r in rel[1:] if r[0] == 0 or r[1] == 0]
    corner_blocks = [r for r in rel[1:] if r[0] != 0 and r[1] != 0]
    for dz in range(nz):
        if dz > 0:
            product(dz, (0, 0))
        for rc in line_blocks:
            product(dz, rc)
        corners(dz)
        if dz + 1 < nz:
            middle(dz + 1)
            if dz + 3 < nz:
                along_z(dz + 3)
        for rc in corner_blocks:
            product(dz, rc)
        bins_of(dz)
        if dz + 1 < nz:
            lines(dz + 1)
            if dz + 2 < nz:
                enter(dz + 2)
            policy(dz)
            pair_sum(dz)
    pair_sum(nz - 1)
    policy(nz - 1)

    width = grad_out.shape[0]
    start = (b * n + c) * width
    aligned = (start // 128) * 128
    gc = aligned // cols
    goff = pl.multiple_of(aligned % cols, 128)
    xt = xbuf[:, gc, :, :, pl.ds(goff, 128)].reshape(nb * rows, 128).T

    logits = psum[0]
    for d in range(1, nz):
        recv(rz.at[d], qs.at[d], qr.at[d])
        logits = logits + rz[d]
    col = iota(logits.shape, 1)
    real = col < bins_n
    logits = jnp.where(real, logits, -jnp.inf)
    e = jnp.exp(logits - jnp.max(logits, axis=-1, keepdims=True))
    bins = -20.0 + 40.0 * col.astype(f32) / (bins_n - 1)
    value = jnp.sum(e * bins, axis=-1, keepdims=True) / jnp.sum(e, axis=-1, keepdims=True)
    shape = (traj, horizon, 128)
    wide = jnp.broadcast_to(value, (rows, 128)).reshape(shape)
    wide = jnp.where(iota(shape, 2) == iota(shape, 1), wide, 0.0)
    v = jnp.sum(wide, axis=1)
    vown[...] = v
    for i, rc in enumerate(rel[1:]):
        back = ((-rc[0]) % ny) * nx + (-rc[1]) % nx
        send(vown, vbuf.at[back], vs.at[i + 1], vr.at[back], (b, crit(*rc)))
    pay[0] = v
    heats = [-v / smoothing_heat_factor]
    for i in range(1, n):
        recv(vbuf.at[i], vs.at[i], vr.at[i])
        heats.append(-vbuf[i] / smoothing_heat_factor)
    top = functools.reduce(jnp.maximum, heats)
    mean = functools.reduce(jnp.add, [jnp.exp(h - top) for h in heats]) / n
    pay[1] = -smoothing_heat_factor * (top + jnp.log(mean))
    for d in range(1, nb):
        send(pay, sbuf.at[b], bs.at[d], br.at[d], batch_peer(d))
    sbuf[b] = pay[...]
    for d in range(1, nb):
        recv(sbuf.at[(b + nb - d) % nb], bs.at[d], br.at[d])
    values = sbuf[:, 0].reshape(total, 128)
    soft = sbuf[:, 1].reshape(total, 128)

    lane = iota((total, 128), 1)
    step = lane.astype(f32)
    mg = metag[...]
    end = mg[:, 2 * horizon : 2 * horizon + 1]
    live = ((step < end) & (lane < horizon)).astype(f32)
    carry = (step + 1.0 < end).astype(f32)

    def ahead(a, s):
        return pltpu.roll(a, 128 - s, 1)

    decay = future_decay_factor * carry
    inner = lane < horizon - 1
    offset = jnp.where(
        inner,
        mg + decay * (1.0 - blend) * ahead(soft, 1),
        jnp.where(lane == horizon - 1, soft, 0.0),
    )
    factor = jnp.where(inner, decay * blend, 0.0)
    s = 1
    while s < horizon:
        offset = offset + factor * ahead(offset, s)
        factor = factor * ahead(factor, s)
        s *= 2
    raw = jnp.where(lane < horizon, (offset - soft) * live, 0.0)
    square = jnp.sum(jnp.sum(raw * raw, axis=1, keepdims=True), axis=0, keepdims=True)
    lives = jnp.sum(jnp.sum(live, axis=1, keepdims=True), axis=0, keepdims=True)
    scale = jnp.sqrt(square / lives + 1e-06)
    adv = raw / scale

    pull = pm[...].reshape(nb * rows, pm.shape[2]) * spread_rows(adv, 0) / horizon
    grad = jnp.dot(xt, pull.astype(bf16), preferred_element_type=f32)
    if width == 128:
        grad_out[...] = grad
    else:
        gtmp[...] = grad
        grad_out[...] = gtmp[pl.ds(pl.multiple_of(start % 128, width), width), :]
    cv_out[0] = jnp.dot(pick_mine, values, preferred_element_type=f32, precision=HIGHEST)[:, 0:horizon]
    adv_out[...] = jnp.dot(pick_mine, adv, preferred_element_type=f32, precision=HIGHEST)[:, 0:horizon]
    for d in sends:
        d.wait_send()


def plane_kernel(
    sizes, lat, dest, ends, rewards, actions, w_hbm, b_in, w_out, aw_hbm,
    cv_out, adv_out, grad_out,
    xbuf, wv, wov, acc, pm, lg, psum, rsib, rz, meta, metabuf, metag,
    vown, vbuf, pay, sbuf,
    wsem, lsem, zs, zr, xs, xr, ss, sr, ps, pr, qs, qr, ms, mr, vs, vr, bs, br,
):
    nb, n, horizon, bins_n = sizes
    nz = nb // 2
    rows, cols = lat.shape
    half = rows // 2
    traj = rows // horizon
    total = nb * traj
    hidden_n = w_hbm.shape[1]
    acts = aw_hbm.shape[1]
    b = lax.axis_index("batch")
    c = lax.axis_index("critic")
    z, k = b // 2, b % 2
    y, x = c // 2, c % 2
    sib = z * 2 + (1 - k)
    col = [c, y * 2 + (1 - x), (1 - y) * 2 + x, (1 - y) * 2 + (1 - x)]
    sends = []

    def closeness(i):
        side = 1 if i < nz / 2 else -1
        return sorted(range(nz), key=lambda p: (abs(p - i), side * (i - p)))

    def pick(values):
        v = jnp.int32(values[0])
        for i in range(1, nz):
            v = jnp.where(z == i, jnp.int32(values[i]), v)
        return v

    orders = [closeness(i) for i in range(nz)]
    plane = [z] + [pick([orders[i][s] for i in range(nz)]) for s in range(1, nz)]

    def batch_peer(d):
        return ((b + d) % nb, c)

    def wcopy(q):
        at = pl.ds(pl.multiple_of(col[q] * cols, cols), cols)
        return (
            pltpu.make_async_copy(
                w_hbm.at[at], wv.at[at, pl.ds(0, hidden_n)], wsem.at[q]
            ),
            pltpu.make_async_copy(
                aw_hbm.at[at], wv.at[at, pl.ds(hidden_n, acts)], wsem.at[4 + q]
            ),
        )

    for d in wcopy(0):
        d.start()
    own_copy = pltpu.make_async_copy(lat, xbuf.at[z, c, k], lsem.at[0])
    own_copy.start()

    below, above = z > 0, z < nz - 1
    barrier = pltpu.get_barrier_semaphore()

    def greet(dev):
        pl.semaphore_signal(barrier, inc=1, device_id=dev, device_id_type=MESH)

    greet((sib, c))
    greet((b, col[1]))
    greet((b, col[2]))

    @pl.when(below)
    def _():
        greet(((z - 1) * 2 + k, c))

    @pl.when(above)
    def _():
        greet(((z + 1) * 2 + k, c))

    pl.semaphore_wait(barrier, 3 + jnp.where(below, 1, 0) + jnp.where(above, 1, 0))

    def send(src, dst, s, r, dev, when=None):
        d = pltpu.make_async_remote_copy(
            src_ref=src, dst_ref=dst, send_sem=s, recv_sem=r, device_id=dev, device_id_type=MESH
        )
        if when is None:
            d.start()
        else:
            pl.when(when)(d.start)
        sends.append((d, when))

    def recv(dst, s, r):
        pltpu.make_async_remote_copy(
            src_ref=dst, dst_ref=dst, send_sem=s, recv_sem=r,
            device_id=(sib, c), device_id_type=MESH,
        ).wait_recv()

    def hrow(h):
        return pl.ds(h * half, half)

    def block(s, q, h=None):
        if h is None:
            return xbuf.at[plane[s], col[q], k]
        return xbuf.at[plane[s], col[q], k, hrow(h)]

    def across(s, h):
        src = lat.at[hrow(h)] if s == 0 else block(s, 0, h)
        for j in (1, 2):
            i = (s * 3 + (j - 1)) * 2 + h
            send(src, block(s, 0, h), xs.at[i], xr.at[i], (b, col[j]))

    def onward(s):
        for j in (1, 2):
            i = (s * 3 + 2) * 2 + (j - 1)
            at = block(s, 3 - j, j - 1)
            send(at, at, xs.at[i], xr.at[i], (b, col[j]))

    def arrived(s, q):
        for h in range(2):
            i = (s * 3 + (q - 1)) * 2 + h
            recv(block(s, q, h), xs.at[0], xr.at[i])

    def relay(s, q):
        src = lat if s == 0 and q == 0 else block(s, q)
        send(src, block(s, q), ss.at[s * 4 + q], sr.at[s * 4 + q], (sib, c))

    def along(h):
        for j, (dz, ok) in enumerate(((-1, below), (1, above))):
            send(
                lat.at[hrow(h)], xbuf.at[z, c, k, hrow(h)],
                zs.at[j * 2 + h], zr.at[z * 2 + h], ((z + dz) * 2 + k, c), ok,
            )

    def passed(d, h):
        for j, sg in enumerate((-1, 1)):
            p = z + sg * d
            there = (p >= 0) & (p < nz)
            on = z - sg
            at = xbuf.at[p, c, k, hrow(h)]

            @pl.when(there)
            def _():
                recv(at, zs.at[0], zr.at[p * 2 + h])

            if d < nz - 1:
                send(
                    at, at, zs.at[(d * 2 + j) * 2 + h], zr.at[p * 2 + h],
                    (on * 2 + k, c), there & (on >= 0) & (on < nz),
                )

    def product(s, q, first=False):
        p, cc = plane[s], col[q]
        recv(xbuf.at[p, cc, 1 - k], ss.at[0], sr.at[s * 4 + q])
        wrows = pl.ds(pl.multiple_of(cc * cols, cols), cols)

        v = jnp.dot(
            xbuf[p, cc].reshape(2 * rows, cols), wv[wrows, :], preferred_element_type=f32
        )
        if first:
            acc[s] = v
        else:
            acc[s] += v

    def bins_of(s):
        hid = jax.nn.silu(acc[s, :, 0:hidden_n] + b_in[...]).astype(bf16)
        v = jnp.dot(hid, wov[...], preferred_element_type=f32)
        lg[s] = v.reshape(2, rows, wov.shape[1])
        send(lg.at[s, 1 - k], rsib.at[s], ps.at[s], pr.at[s], (sib, c))

    def pair_sum(s):
        recv(rsib.at[s], ps.at[s], pr.at[s])
        psum[s] = lg[s, k] + rsib[s]
        if s > 0:
            send(psum.at[s], rz.at[z], qs.at[s], qr.at[z], (plane[s] * 2 + k, c))

    def spread_rows(m, base):
        t = m.shape[0]
        shape = (t, horizon, m.shape[1])
        keep = iota(shape, 2) == iota(shape, 1) + base
        wide = jnp.where(keep, jnp.broadcast_to(m[:, None, :], shape), 0.0)
        return jnp.sum(wide.reshape(t * horizon, m.shape[1]), axis=-1, keepdims=True)

    def policy(s):
        p = plane[s]
        l = acc[s, :, hidden_n : hidden_n + acts]
        e = jnp.exp(l - jnp.max(l, axis=-1, keepdims=True))
        prob = e / jnp.sum(e, axis=-1, keepdims=True)
        m = metag[pl.ds(pl.multiple_of(p * 2 * traj, 2 * traj), 2 * traj), :]
        a = spread_rows(m, horizon)
        hot = (iota(l.shape, 1).astype(f32) == a).astype(f32)
        pm[p] = prob - hot

    along(0)
    across(0, 0)
    relay(0, 0)
    along(1)
    across(0, 1)
    for q in range(1, 4):
        for d in wcopy(q):
            d.start()

    row = iota((traj, 128), 0)
    lane = iota((traj, 128), 1)
    m = jnp.zeros((traj, 128), f32)
    for i in range(traj):
        m = jnp.where((row == i) & (lane == 2 * horizon), ends[i].astype(f32), m)
        m = jnp.where((row == i) & (lane == 2 * horizon + 1), dest[i].astype(f32), m)
    meta[...] = m
    meta[:, 0:horizon] = rewards[...]
    meta[:, horizon : 2 * horizon] = actions[...].astype(f32)
    metabuf[b] = meta[...]
    wov[...] = jnp.zeros_like(wov)
    wov[:, 0:bins_n] = w_out[...]

    def ready(q):
        for d in wcopy(q):
            d.wait()

    own_copy.wait()
    ready(0)
    product(0, 0, True)
    for q in range(1, 4):
        ready(q)
    passed(1, 0)
    across(1, 0)
    passed(1, 1)
    across(1, 1)
    relay(1, 0)
    for q in (1, 2):
        arrived(0, q)
        relay(0, q)
    for s in range(2, nz):
        product(s - 1, 0, True)
        product(s - 2, 1)
        passed(s, 0)
        across(s, 0)
        product(s - 2, 2)
        passed(s, 1)
        across(s, 1)
        relay(s, 0)
        for q in (1, 2):
            arrived(s - 1, q)
            relay(s - 1, q)
    order = [nz - 2] + list(range(1, nz - 2)) + [nz - 1, 0]
    for s in order[:-2]:
        onward(s)
    product(nz - 1, 0, True)
    for d in range(1, nb):
        send(meta, metabuf.at[b], ms.at[d], mr.at[d], batch_peer(d))
    for q in (1, 2):
        product(nz - 2, q)
    for q in (1, 2):
        arrived(nz - 1, q)
        relay(nz - 1, q)
    onward(nz - 1)
    onward(0)

    for d in range(1, nb):
        recv(metabuf.at[(b + nb - d) % nb], ms.at[d], mr.at[d])
    everyone = metabuf[...].reshape(total, 128)
    dest_all = everyone[:, 2 * horizon + 1 : 2 * horizon + 2]
    pickm = (iota((total, total), 1).astype(f32) == dest_all).astype(f32)
    metag[...] = jnp.dot(pickm, everyone, preferred_element_type=f32, precision=HIGHEST)
    mine = (iota((traj, total), 1) == iota((traj, total), 0) + b * traj).astype(f32)
    pick_mine = lax.dot_general(
        mine, pickm, (((1,), (1,)), ((), ())), preferred_element_type=f32
    )
    for q in (1, 2):
        product(nz - 1, q)

    before = None
    for s in order:
        arrived(s, 3)
        relay(s, 3)
        if before is not None:
            pair_sum(before)
        product(s, 3)
        bins_of(s)
        if s != order[-1]:
            policy(s)
        before = s
    policy(before)
    gc = ((b * n + c) * grad_out.shape[0]) // cols
    goff = pl.multiple_of(((b * n + c) * grad_out.shape[0]) % cols, 128)
    xt = xbuf[:, gc, :, :, pl.ds(goff, 128)].reshape(nb * rows, 128).T
    pair_sum(before)

    logits = psum[0]
    for d in range(1, nz):
        o = (z + d) % nz
        recv(rz.at[o], qs.at[0], qr.at[o])
        logits = logits + rz[o]
    lane2 = iota(logits.shape, 1)
    real = lane2 < bins_n
    logits = jnp.where(real, logits, -jnp.inf)
    e = jnp.exp(logits - jnp.max(logits, axis=-1, keepdims=True))
    bins = -20.0 + 40.0 * lane2.astype(f32) / (bins_n - 1)
    value = jnp.sum(e * bins, axis=-1, keepdims=True) / jnp.sum(e, axis=-1, keepdims=True)
    shape = (traj, horizon, 128)
    wide = jnp.broadcast_to(value, (rows, 128)).reshape(shape)
    wide = jnp.where(iota(shape, 2) == iota(shape, 1), wide, 0.0)
    v = jnp.sum(wide, axis=1)
    vown[...] = v
    for i in range(1, n):
        send(vown, vbuf.at[i], vs.at[i], vr.at[i], (b, col[i]))
    pay[0] = v
    heats = [-v / smoothing_heat_factor]
    for i in range(1, n):
        recv(vbuf.at[i], vs.at[i], vr.at[i])
        heats.append(-vbuf[i] / smoothing_heat_factor)
    top = functools.reduce(jnp.maximum, heats)
    mean = functools.reduce(jnp.add, [jnp.exp(h - top) for h in heats]) / n
    pay[1] = -smoothing_heat_factor * (top + jnp.log(mean))
    for d in range(1, nb):
        send(pay, sbuf.at[b], bs.at[d], br.at[d], batch_peer(d))
    sbuf[b] = pay[...]
    for d in range(1, nb):
        recv(sbuf.at[(b + nb - d) % nb], bs.at[d], br.at[d])
    values = sbuf[:, 0].reshape(total, 128)
    soft = sbuf[:, 1].reshape(total, 128)

    lane = iota((total, 128), 1)
    step = lane.astype(f32)
    mg = metag[...]
    end = mg[:, 2 * horizon : 2 * horizon + 1]
    live = ((step < end) & (lane < horizon)).astype(f32)
    carry = (step + 1.0 < end).astype(f32)

    def ahead(a, s):
        return pltpu.roll(a, 128 - s, 1)

    decay = future_decay_factor * carry
    inner = lane < horizon - 1
    offset = jnp.where(
        inner,
        mg + decay * (1.0 - blend) * ahead(soft, 1),
        jnp.where(lane == horizon - 1, soft, 0.0),
    )
    factor = jnp.where(inner, decay * blend, 0.0)
    s = 1
    while s < horizon:
        offset = offset + factor * ahead(offset, s)
        factor = factor * ahead(factor, s)
        s *= 2
    raw = jnp.where(lane < horizon, (offset - soft) * live, 0.0)
    square = jnp.sum(jnp.sum(raw * raw, axis=1, keepdims=True), axis=0, keepdims=True)
    lives = jnp.sum(jnp.sum(live, axis=1, keepdims=True), axis=0, keepdims=True)
    scale = jnp.sqrt(square / lives + 1e-06)
    adv = raw / scale

    pull = pm[...].reshape(nb * rows, pm.shape[2]) * spread_rows(adv, 0) / horizon
    grad_out[...] = jnp.dot(xt, pull.astype(bf16), preferred_element_type=f32)
    cv_out[0] = jnp.dot(pick_mine, values, preferred_element_type=f32, precision=HIGHEST)[:, 0:horizon]
    adv_out[...] = jnp.dot(pick_mine, adv, preferred_element_type=f32, precision=HIGHEST)[:, 0:horizon]
    for d, when in sends:
        if when is None:
            d.wait_send()
        else:
            pl.when(when)(d.wait_send)


def hand_over(cv, adv, grad, cv_out, adv_out, grad_out):
    cv_out[...] = cv[...]
    adv_out[...] = adv[...]
    grad_out[...] = grad[...]


def on_planes(latents, dest, ends, rewards, actions, w_in, b_in, w_out, actor_w):
    nb = lax.axis_size("batch")
    n = lax.axis_size("critic")
    traj, horizon, cols = latents.shape
    rows = traj * horizon
    width, hidden_n = w_in.shape[1:]
    bins_n = w_out.shape[2]
    acts = actor_w.shape[1]
    nz = nb // 2
    lanes = -(-bins_n // 128) * 128
    vmem = pltpu.VMEM
    dma = pltpu.SemaphoreType.DMA
    scratch = [
        vmem((nz, n, 2, rows, cols), bf16),
        vmem((width, hidden_n + acts), bf16),
        vmem((hidden_n, lanes), bf16),
        vmem((nz, 2 * rows, hidden_n + acts), f32),
        vmem((nz, 2 * rows, acts), f32),
        vmem((nz, 2, rows, lanes), f32),
        vmem((nz, rows, lanes), f32),
        vmem((nz, rows, lanes), f32),
        vmem((nz, rows, lanes), f32),
        vmem((traj, 128), f32),
        vmem((nb, traj, 128), f32),
        vmem((nb * traj, 128), f32),
        vmem((traj, 128), f32),
        vmem((n, traj, 128), f32),
        vmem((2, traj, 128), f32),
        vmem((nb, 2, traj, 128), f32),
        dma((2 * n,)), dma((1,)),
        dma((nz * 4,)), dma((nz * 2,)),
        dma((nz * 6,)), dma((nz * 6,)),
        dma((nz * n,)), dma((nz * n,)),
        dma((nz,)), dma((nz,)),
        dma((nz,)), dma((nz,)),
        dma((nb,)), dma((nb,)),
        dma((n,)), dma((n,)),
        dma((nb,)), dma((nb,)),
    ]
    inside = pl.BlockSpec(memory_space=pltpu.VMEM)
    scalar = pl.BlockSpec(memory_space=pltpu.SMEM)
    outside = pl.BlockSpec(memory_space=pl.ANY)
    shapes = (
        jax.ShapeDtypeStruct((1, traj, horizon), f32),
        jax.ShapeDtypeStruct((traj, horizon), f32),
        jax.ShapeDtypeStruct((width // (nb * n), acts), f32),
    )
    out = pl.pallas_call(
        functools.partial(plane_kernel, (nb, n, horizon, bins_n)),
        out_shape=shapes,
        in_specs=[outside, scalar, scalar, inside, inside, outside, inside, inside, outside],
        out_specs=(inside, inside, inside),
        scratch_shapes=scratch,
        compiler_params=pltpu.CompilerParams(
            collective_id=0, has_side_effects=True, vmem_limit_bytes=60 * 1024 * 1024
        ),
    )(
        latents.reshape(rows, cols), dest, ends, rewards, actions,
        w_in[0], b_in, w_out[0], actor_w,
    )
    return pl.pallas_call(
        hand_over, out_shape=shapes, in_specs=[inside] * 3, out_specs=(inside,) * 3
    )(*out)


def on_device(latents, dest, ends, rewards, actions, w_in, b_in, w_out, actor_w):
    nb = lax.axis_size("batch")
    n = lax.axis_size("critic")
    traj, horizon, cols = latents.shape
    rows = traj * horizon
    width, hidden_n = w_in.shape[1:]
    bins_n = w_out.shape[2]
    acts = actor_w.shape[1]
    nx = 1
    while nx * nx * 4 <= n:
        nx *= 2
    ny = n // nx
    if nx * nx < n and nx == 1:
        nx, ny = n, 1
    nz = nb // 2
    lanes = -(-bins_n // 128) * 128
    half_sends = nz * (2 * (nx - 1 + ny - 1) + 2 * (nx - 1) * (ny - 1))
    vmem = pltpu.VMEM
    dma = pltpu.SemaphoreType.DMA
    scratch = [
        vmem((nz, n, 2, rows, cols), bf16),
        vmem((width, hidden_n), bf16),
        vmem((width, acts), bf16),
        vmem((hidden_n, lanes), bf16),
        vmem((2 * rows, hidden_n), f32),
        vmem((nz, 2 * rows, acts), f32),
        vmem((nz, 2, rows, lanes), f32),
        vmem((nz, rows, lanes), f32),
        vmem((nz, rows, lanes), f32),
        vmem((nz, rows, lanes), f32),
        vmem((traj, 128), f32),
        vmem((nb, traj, 128), f32),
        vmem((nb * traj, 128), f32),
        vmem((traj, 128), f32),
        vmem((n, traj, 128), f32),
        vmem((2, traj, 128), f32),
        vmem((nb, 2, traj, 128), f32),
        vmem((128, acts), f32),
        dma((n,)), dma((2,)),
        dma((nz,)), dma((nz,)),
        dma((half_sends,)), dma((nz * n * 2,)),
        dma((nz * n,)), dma((nz * n,)),
        dma((nz,)), dma((nz,)),
        dma((nz,)), dma((nz,)),
        dma((nb,)), dma((nb,)),
        dma((n,)), dma((n,)),
        dma((nb,)), dma((nb,)),
    ]
    inside = pl.BlockSpec(memory_space=pltpu.VMEM)
    scalar = pl.BlockSpec(memory_space=pltpu.SMEM)
    outside = pl.BlockSpec(memory_space=pl.ANY)
    return pl.pallas_call(
        functools.partial(kernel, (nb, n, ny, nx, horizon, bins_n)),
        out_shape=(
            jax.ShapeDtypeStruct((1, traj, horizon), f32),
            jax.ShapeDtypeStruct((traj, horizon), f32),
            jax.ShapeDtypeStruct((width // (nb * n), acts), f32),
        ),
        in_specs=[outside, scalar, scalar, inside, inside, outside, inside, inside, outside],
        out_specs=(inside, inside, inside),
        scratch_shapes=scratch,
        compiler_params=pltpu.CompilerParams(
            collective_id=0, has_side_effects=True, vmem_limit_bytes=60 * 1024 * 1024
        ),
    )(
        latents.reshape(rows, cols), dest, ends, rewards, actions,
        w_in[0], b_in, w_out[0], actor_w,
    )


def solution(mesh):
    placed = (
        P("batch", None, "critic"),
        P("batch"),
        P("batch"),
        P("batch", None),
        P("batch", None),
        P("critic", None, "batch"),
        P("critic", "batch"),
        P("critic", "batch", None),
        P(),
    )
    planes = mesh.shape["batch"] == 8 and mesh.shape["critic"] == 4
    return jax.shard_map(
        on_planes if planes else on_device,
        mesh=mesh,
        in_specs=placed,
        out_specs=(P("critic", "batch", None), P("batch", None), P(("batch", "critic"), None)),
        check_vma=False,
    )
```
